256 devices in a mesh: rep: 8 (over z), ep: 32 (over x, y, core).
Axes of the slice: x: 4, y: 4, z: 8, core: 2. Of those that a mesh axis runs over, the one named last changes fastest.
Arguments:
- hidden_in: bfloat16 [32768, 2048], P(('rep', 'ep')), may hold values from -3 to 3
- tree_queries: bfloat16 [32768, 2048], P(('rep', 'ep')), may hold values from -6 to 6
- tree_keys: bfloat16 [32768, 2048], P(('rep', 'ep')), may hold values from -6 to 6
- tree_values: bfloat16 [32768, 2048], P(('rep', 'ep')), may hold values from -12 to 12
- tree_parents: int32 [512, 64], P(('rep', 'ep')), may hold values from -1 to 62, as said below
- accepted_nodes: int32 [512, 16], P(('rep', 'ep')), may hold values from 0 to 63
- request_prompt: int32 [512], P(('rep', 'ep')), may hold values from 0 to 3
- prompt_lengths: int32 [32], P('rep'), may hold values from 24 to 192, as said below
- prompt_keys: bfloat16 [32, 192, 2048], P('rep', 'ep'), may hold values from -6 to 6
- prompt_values: bfloat16 [32, 192, 2048], P('rep', 'ep'), may hold values from -12 to 12
- out_proj: bfloat16 [2048, 2048], P('rep'), may hold values from -0.125 to 0.125
- norm_gain: float32 [2048], replicated, may hold values from 0.1 to 1.9
- expert_ids: int32 [32768, 8], P(('rep', 'ep')), may hold values from 0 to 31, all different within a row; in each aligned block of 128 rows (0 to 127, 128 to 255, ...) at most 40 rows name the same one
- gate_weights: float32 [32768, 8], P(('rep', 'ep')), may hold values from 0.05 to 0.5
- expert_gate_up: bfloat16 [32, 2048, 1024], P('ep'), may hold values from -0.125 to 0.125
- expert_down: bfloat16 [32, 512, 2048], P('ep'), may hold values from -0.25 to 0.25
Outputs:
- layer_out: bfloat16 [32768, 2048], P(('rep', 'ep'))
- accepted_cache: bfloat16 [512, 16, 4096], P(('rep', 'ep'))
The draws below stay inside these ranges and needn't reach their ends.
Inputs may be any that keep to these rules, and one draw needn't show every extreme that they name: `tree_parents`: node 0 of every request has parent -1; every other node's parent is one of the 8 nodes before it. `request_prompt`: index of the request's prompt among the 4 prompts of its index of rep. `prompt_lengths`: among the 4 prompts of each index of rep, one has all 192 positions. `expert_ids`: each row names 8 different experts; on the rows of one device no expert is named by more than 40 rows.
All inputs are finite; a program needn't handle non-finite values.
Results may differ from the reference program's by a relative error of at most 0.012.
Values may be sent and summed in bfloat16 or wider, within the bound.
A program may use at most 128 MiB of HBM per device.

```python
import math
import jax
import jax.numpy as jnp
import numpy as np
from jax import lax

D = 2048
HEADS = 16
HEAD_DIM = 128
TOP = 8
EXPERTS = 32
FF_WIN = 512
TREE = 64
PLEN = 192
PROMPTS = 4
CAP = 40
PATH = 16
TOK_DEV = 128
REQ_ROW = 64
REQUESTS = 512
TOKENS = 32768
GROUPS = 32
N_REP = 8
N_EP = 32


def tree_links(key):
    link_key = jax.random.fold_in(key, 3)
    node_ids = jnp.arange(TREE, dtype=jnp.int32)
    spread = jnp.minimum(jnp.maximum(node_ids, 1), 8)
    random_bits = jax.random.randint(link_key, (REQUESTS, TREE), 0, 65536, dtype=jnp.int32)
    parents = node_ids[None, :] - 1 - random_bits % spread[None, :]
    return jnp.where(node_ids[None, :] == 0, -1, parents).astype(jnp.int32)


def draw_tree_parents(key, part):
    return tree_links(key)


def draw_tree_queries(key, part):
    drawn_rows = jnp.clip(jax.random.normal(jax.random.fold_in(key, 21), (TOKENS, D), jnp.float32), -5.0, 5.0)
    return drawn_rows.astype(jnp.bfloat16)


def draw_tree_keys(key, part):
    drawn_rows = jnp.clip(jax.random.normal(jax.random.fold_in(key, 23), (TOKENS, D), jnp.float32), -5.0, 5.0)
    return drawn_rows.astype(jnp.bfloat16)


def draw_prompt_lengths(key, part):
    rows_count = GROUPS // PROMPTS
    drawn_lengths = jax.random.randint(jax.random.fold_in(key, 5), (rows_count, PROMPTS), PLEN // 8, PLEN + 1, dtype=jnp.int32)
    longest = jax.random.randint(jax.random.fold_in(key, 6), (rows_count, 1), 0, PROMPTS, dtype=jnp.int32)
    drawn_lengths = jnp.where(jnp.arange(PROMPTS, dtype=jnp.int32)[None, :] == longest, PLEN, drawn_lengths)
    return drawn_lengths.reshape(-1).astype(jnp.int32)


def set_ends(values, stream_key, low, largest):
    longest = values.shape.index(max(values.shape))
    spots = []
    for shift in (0, 1):
        where = [jax.random.randint(jax.random.fold_in(stream_key, axis), (), 0, length) for axis, length in enumerate(values.shape)]
        where[longest] = (where[longest] + shift) % values.shape[longest]
        spots.append(tuple(where))
    return values.at[spots[0]].set(low).at[spots[1]].set(largest)


def shard_levels(key, extent, pieces, low, largest):
    def one(position, shards_of):
        draws = jax.random.uniform(jax.random.fold_in(jax.random.fold_in(key, 6), position), (shards_of,), jnp.float32, low / len(pieces), largest / len(pieces))
        return jnp.repeat(jnp.exp(draws), extent[position] // shards_of).reshape((-1,) + (1,) * (len(extent) - position - 1))

    level = one(*pieces[0])
    for cut in pieces[1:]:
        level = level * one(*cut)
    return level


def assign_block(rng, own, number, rows, number_of, top, reach, lean):
    ranking = jax.random.permutation(rng, number_of)
    packed, usual = shares(number_of, rows * top, reach, lean, True), shares(number_of, rows * top, reach, lean, False)
    places = jnp.arange(number_of)

    def named(lengths, turn):
        used = int((lengths > 0).sum())
        fixed = max(1, used // 4)
        shifted = fixed + (places - fixed + turn * (used - fixed)) % max(1, number_of - fixed)
        return jnp.zeros((number_of,), jnp.int32).at[ranking[jnp.where(places < fixed, places, shifted)]].set(jnp.asarray(lengths, jnp.int32))

    lengths = jnp.where(number % 4 == 0, named(packed, number // 4), named(usual, number - number // 4 - 1))
    mixed = jax.random.permutation(jax.random.fold_in(own, 3), number_of)
    source_of, receiver = mixed[0:number_of // 2 * 2:2], mixed[1:number_of // 2 * 2:2]
    slack = jnp.minimum(lengths[source_of] - 1, reach - lengths[receiver]) // 2
    slack = jnp.where((source_of == ranking[0]) | (receiver == ranking[0]) | (lengths[receiver] == 0), 0, jnp.maximum(slack, 0))
    shifted = jax.random.randint(jax.random.fold_in(own, 4), (number_of // 2,), 0, 1 << 20) % (slack + 1)
    lengths = lengths.at[source_of].add(-shifted).at[receiver].add(shifted)
    members = jnp.searchsorted(jnp.cumsum(lengths), jnp.arange(rows * top), side="right").astype(jnp.int32)
    grid = members.reshape(top, rows).T
    grid = grid[jax.random.permutation(jax.random.fold_in(own, 1), rows)]
    turn = jax.random.randint(jax.random.fold_in(own, 2), (rows, 1), 0, top)
    return jnp.take_along_axis(grid, (jnp.arange(top)[None, :] + turn) % top, axis=1)


def shares(count, total, limit, lean, full):
    portions = [(1 << 20) // math.isqrt(rank ** lean) + 1 for rank in range(1, count + 1)]
    largest = limit if full else min(limit, max(-(-total // count), total * portions[0] // sum(portions)))
    least = 1 if total - largest >= count - 1 else 0
    holding, surplus = [largest] + [least] * (count - 1), total - largest - least * (count - 1)
    while surplus > 0:
        candidates = [i for i in range(1, count) if holding[i] < largest] or [i for i in range(1, count) if holding[i] < limit]
        pool, budget = sum([portions[i] for i in candidates]), surplus
        for i in candidates:
            more = min(limit - holding[i], max(1, budget * portions[i] // pool), surplus)
            holding[i] = holding[i] + more
            surplus = surplus - more
    return np.array(holding)


def noise(own_key, extent, deviation, limit, shards=(), kind=jnp.bfloat16):
    result = deviation * jax.random.normal(own_key, extent, jnp.float32)
    if shards:
        result = result * shard_levels(own_key, extent, shards, -0.22, 0.18)
    return jnp.clip(result, -limit, limit).astype(kind)


def setup_inputs(seed: int = 0) -> dict:
    streams_of = jax.random.split(jax.random.key(seed), 17)
    hidden_in = noise(streams_of[0], (TOKENS, D), 0.5, 3.0, ((0, 256),))
    tree_queries = draw_tree_queries(jax.random.fold_in(streams_of[16], 71), 0)
    tree_keys = draw_tree_keys(jax.random.fold_in(streams_of[16], 71), 0)
    tree_values = noise(streams_of[3], (TOKENS, D), 2.0, 12.0, ((0, 256),))
    tree_parents = draw_tree_parents(jax.random.fold_in(streams_of[16], 71), 0)
    accepted_nodes = set_ends(jax.random.randint(streams_of[5], (REQUESTS, PATH), 0, TREE), jax.random.fold_in(streams_of[5], 1), 0, TREE - 1).astype(jnp.int32)
    request_prompt = set_ends(jax.random.randint(streams_of[6], (REQUESTS,), 0, PROMPTS), jax.random.fold_in(streams_of[6], 1), 0, PROMPTS - 1).astype(jnp.int32)
    prompt_lengths = draw_prompt_lengths(jax.random.fold_in(streams_of[16], 71), 0)
    prompt_keys = noise(streams_of[8], (GROUPS, PLEN, D), 1.0, 6.0, ((0, 8), (1, 32)))
    prompt_values = noise(streams_of[9], (GROUPS, PLEN, D), 2.0, 12.0, ((0, 8), (1, 32)))
    out_proj = noise(streams_of[10], (D, D), D ** -0.5, 0.125, ((0, 8),))
    norm_gain = jnp.clip(1.0 + 0.18 * jax.random.normal(streams_of[11], (D,), jnp.float32), 0.1, 1.9)
    expert_ids_keys = jax.random.split(jax.random.fold_in(streams_of[12], 1), TOKENS // TOK_DEV)
    expert_ids_turns = jax.random.permutation(jax.random.fold_in(streams_of[12], 3), TOKENS // TOK_DEV)
    expert_ids = jax.vmap(lambda own, number: assign_block(jax.random.fold_in(streams_of[12], 2), own, number, TOK_DEV, EXPERTS, TOP, CAP, 2))(expert_ids_keys, expert_ids_turns).reshape((TOKENS, TOP))
    gate_weights = jnp.clip(jnp.exp(math.log(0.5) - 2.3025851 * jax.random.uniform(streams_of[13], (TOKENS, TOP), jnp.float32) ** shard_levels(streams_of[13], (TOKENS, TOP), ((0, 256),), -0.2, 0.2)), 0.05, 0.5)
    expert_gate_up = noise(streams_of[14], (EXPERTS, D, 2 * FF_WIN), D ** -0.5, 0.125, ((0, 32),))
    expert_down = noise(streams_of[15], (EXPERTS, FF_WIN, D), FF_WIN ** -0.5, 0.25, ((0, 32),))
    return {"hidden_in": hidden_in, "tree_queries": tree_queries, "tree_keys": tree_keys, "tree_values": tree_values, "tree_parents": tree_parents, "accepted_nodes": accepted_nodes, "request_prompt": request_prompt, "prompt_lengths": prompt_lengths, "prompt_keys": prompt_keys, "prompt_values": prompt_values, "out_proj": out_proj, "norm_gain": norm_gain, "expert_ids": expert_ids, "gate_weights": gate_weights, "expert_gate_up": expert_gate_up, "expert_down": expert_down}


NEG_FILL = -1e+30
EPSILON = 1e-05

def ancestry(parents):
    tree_width = parents.shape[-1]
    node_ids = jnp.arange(tree_width, dtype=jnp.int32)
    linked = jnp.logical_or(parents[..., :, None] == node_ids[None, :], node_ids[:, None] == node_ids[None, :])
    closure = linked.astype(jnp.float32)
    for repeat in range(tree_width.bit_length()):
        closure = jnp.minimum(1.0, jnp.einsum('rij,rjk->rik', closure, closure, precision=lax.Precision.HIGHEST))
    return closure > 0.5

def attend_all(tree_queries, tree_keys, tree_values, tree_parents, request_prompt, prompt_lengths, prompt_keys, prompt_values):
    score_scale = 1.0 / math.sqrt(HEAD_DIM)
    block_size = math.gcd(REQUESTS, 8)

    def one_request(request):
        first_row = request * TREE
        queries = lax.dynamic_slice_in_dim(tree_queries, first_row, TREE, 0).astype(jnp.float32).reshape(TREE, HEADS, HEAD_DIM)
        own_keys = lax.dynamic_slice_in_dim(tree_keys, first_row, TREE, 0).astype(jnp.float32)
        own_values = lax.dynamic_slice_in_dim(tree_values, first_row, TREE, 0).astype(jnp.float32)
        group_index = request // REQ_ROW * PROMPTS + request_prompt[request]
        all_keys = jnp.concatenate([prompt_keys[group_index].astype(jnp.float32), own_keys], axis=0).reshape(PLEN + TREE, HEADS, HEAD_DIM)
        all_values = jnp.concatenate([prompt_values[group_index].astype(jnp.float32), own_values], axis=0).reshape(PLEN + TREE, HEADS, HEAD_DIM)
        tree_seen = ancestry(tree_parents[request][None, :])[0]
        cached_seen = jnp.arange(PLEN, dtype=jnp.int32) < prompt_lengths[group_index]
        visible = jnp.concatenate([jnp.broadcast_to(cached_seen[None, :], (TREE, PLEN)), tree_seen], axis=1)
        scores = jnp.einsum('thd,khd->htk', queries, all_keys) * score_scale
        masked = jnp.where(visible[None], scores, NEG_FILL)
        highest = lax.optimization_barrier(jnp.max(masked, axis=-1, keepdims=True))
        exp_weights = jnp.where(visible[None], jnp.exp(masked - highest), 0.0)
        denominator = lax.optimization_barrier(jnp.sum(exp_weights, axis=-1))
        rounded = lax.optimization_barrier(exp_weights.astype(jnp.bfloat16)).astype(jnp.float32)
        mixed_out = jnp.einsum('htk,khd->thd', rounded, all_values) / jnp.transpose(denominator)[:, :, None]
        return mixed_out.reshape(TREE, D).astype(jnp.bfloat16)
    request_ids = jnp.arange(REQUESTS, dtype=jnp.int32).reshape(REQUESTS // block_size, block_size)
    attended = lax.map(jax.vmap(one_request), request_ids)
    return attended.reshape(TOKENS, D)

def experts_all(normed, expert_ids, gate_weights, expert_gate_up, expert_down):
    flat_ids = expert_ids.reshape(-1)
    ordering = jnp.argsort(flat_ids, stable=True).astype(jnp.int32)
    counts = lax.optimization_barrier(jnp.sum((flat_ids[:, None] == jnp.arange(EXPERTS, dtype=jnp.int32)[None, :]).astype(jnp.int32), axis=0))
    starts = (jnp.cumsum(counts) - counts).astype(jnp.int32)
    row_bound = CAP * N_REP * N_EP
    padded = jnp.concatenate([ordering, jnp.zeros((row_bound,), jnp.int32)])
    flat_gates = gate_weights.reshape(-1)
    hidden_units = expert_down.shape[1]

    def visit(accumulated, expert):
        picked = lax.dynamic_slice_in_dim(padded, starts[expert], row_bound, 0)
        is_valid = jnp.arange(row_bound, dtype=jnp.int32) < counts[expert]
        token_rows = picked // TOP
        inputs = normed[token_rows]
        joint_proj = jnp.dot(inputs, expert_gate_up[expert], preferred_element_type=jnp.float32)
        activated = (jax.nn.silu(joint_proj[:, :hidden_units]) * joint_proj[:, hidden_units:]).astype(jnp.bfloat16)
        produced = jnp.dot(activated, expert_down[expert], preferred_element_type=jnp.float32).astype(jnp.bfloat16)
        weighted = jnp.where(is_valid[:, None], flat_gates[picked][:, None] * produced.astype(jnp.float32), 0.0)
        return (accumulated.at[token_rows].add(weighted), None)
    mixture, unused = lax.scan(visit, jnp.zeros((TOKENS, D), jnp.float32), jnp.arange(EXPERTS, dtype=jnp.int32))
    return mixture

def reference(hidden_in, tree_queries, tree_keys, tree_values, tree_parents, accepted_nodes, request_prompt, prompt_lengths, prompt_keys, prompt_values, out_proj, norm_gain, expert_ids, gate_weights, expert_gate_up, expert_down):
    attended = attend_all(tree_queries, tree_keys, tree_values, tree_parents, request_prompt, prompt_lengths, prompt_keys, prompt_values)
    projected = jnp.dot(attended, out_proj, preferred_element_type=jnp.float32)
    residual = hidden_in.astype(jnp.float32) + projected
    normed = (residual * lax.rsqrt(lax.optimization_barrier(jnp.mean(residual * residual, axis=-1, keepdims=True)) + EPSILON) * norm_gain).astype(jnp.bfloat16)
    mixture = experts_all(normed, expert_ids, gate_weights, expert_gate_up, expert_down)
    layer_out = (residual + mixture).astype(jnp.bfloat16)
    accepted_rows = jnp.arange(REQUESTS, dtype=jnp.int32)[:, None] * TREE + accepted_nodes
    accepted_cache = jnp.concatenate([tree_keys[accepted_rows], tree_values[accepted_rows]], axis=-1)
    return (layer_out, accepted_cache)
```

```python
import math

import jax
import jax.numpy as jnp
from jax import lax
from jax.experimental import pallas as pl
from jax.experimental.pallas import tpu as pltpu
from jax.sharding import PartitionSpec as P

HEADS = 16
HEAD_DIM = 128


NEG_FILL = -1e30
EPSILON = 1e-05


RING = 4
GATE_LANES = 128


def ring_parent(offset, plus):
    if plus:
        return {1: (0, True), 2: (1, True), 3: (0, False)}[offset]
    return {3: (0, False), 2: (3, False), 1: (0, True)}[offset]


def tree_edge(quarter, node):
    first = 0 if quarter < 2 else 1
    plus = quarter % 2 == 0
    axis = 1 - first if node[1 - first] else first
    before, forward = ring_parent(node[axis], plus)
    parent = list(node)
    parent[axis] = before
    return tuple(parent), 2 * axis + (0 if forward else 1)


NODES = [(a, b) for a in range(RING) for b in range(RING) if (a, b) != (0, 0)]


def tree_children():
    children = {}
    for quarter in range(4):
        for node in NODES:
            parent, way = tree_edge(quarter, node)
            children.setdefault((quarter, parent), []).append((node, way))
    return children


CHILDREN = tree_children()


def subtree(quarter, node):
    return 1 + sum(subtree(quarter, child) for child, _ in CHILDREN.get((quarter, node), []))


for _key in CHILDREN:
    CHILDREN[_key].sort(key=lambda item: -subtree(_key[0], item[0]))


def broadcast_plan(hop=0.4):
    free = [0.0] * 4
    first = sorted(
        ((q, node, way) for q in range(4) for node, way in CHILDREN[(q, (0, 0))]),
        key=lambda item: -subtree(item[0], item[1]),
    )
    waiting = []
    for q, node, way in first:
        free[way] += 1.0
        waiting.append((free[way] + hop, q, node))
    arrivals = []
    while waiting:
        waiting.sort()
        now, q, node = waiting.pop(0)
        arrivals.append((q, node, now))
        for child, way in CHILDREN.get((q, node), []):
            free[way] = max(free[way], now) + 1.0
            waiting.append((free[way] + hop, q, child))
    return first, arrivals


OWN_SENDS, ARRIVALS = broadcast_plan()


def block_order():
    done = {}
    for q, node, now in ARRIVALS:
        done[node] = max(done.get(node, 0.0), now)
    return [(0, 0)] + sorted(done, key=lambda node: (done[node], node))


ORDER = block_order()
SLOT = {node: index for index, node in enumerate(ORDER)}


def message(quarter, node):
    return quarter * 15 + node[0] * RING + node[1] - 1


def plane_position():
    rep, ep = lax.axis_index("rep"), lax.axis_index("ep")
    core = ep % 2
    chip = ep // 2
    return rep, chip // RING, chip % RING, core


def neighbours():
    rep, x, y, core = plane_position()

    def device(px, py, pc):
        return (rep, (px * RING + py) * 2 + pc)

    return (
        device((x + 1) % RING, y, core),
        device((x + RING - 1) % RING, y, core),
        device(x, (y + 1) % RING, core),
        device(x, (y + RING - 1) % RING, core),
        device(x, y, 1 - core),
    )


MESH = pl.DeviceIdType.MESH


def greet(devices):
    barrier = pltpu.get_barrier_semaphore()
    for device in devices:
        pl.semaphore_signal(barrier, inc=1, device_id=device, device_id_type=MESH)
    pl.semaphore_wait(barrier, len(devices))


BLOCKS_PER_STEP = 2


def experts_kernel(
    x_ref, res_ref, wgu_ref, wd_ref, out_ref,
    xg, cbuf, rbuf, wgu, wd, hid,
    send_sem, recv_sem, back_send, back_recv, local_sem, pair_send, pair_recv,
):
    rows, wide = x_ref.shape
    width = wide - GATE_LANES
    quarter_rows = rows // 4
    units = wd_ref.shape[0]
    ways = neighbours()
    sibling = ways[4]
    greet(ways)

    def part(q):
        return pl.ds(q * quarter_rows, quarter_rows)

    def forward(src, q, node, way):
        return pltpu.make_async_remote_copy(
            src_ref=src,
            dst_ref=xg.at[SLOT[node], part(q)],
            send_sem=send_sem,
            recv_sem=recv_sem.at[message(q, node)],
            device_id=ways[way],
            device_id_type=MESH,
        )

    for q, node, way in OWN_SENDS:
        forward(x_ref.at[part(q)], q, node, way).start()

    pair = [
        pltpu.make_async_remote_copy(
            src_ref=wgu_ref, dst_ref=wgu.at[1], send_sem=pair_send.at[0],
            recv_sem=pair_recv.at[0], device_id=sibling, device_id_type=MESH,
        ),
        pltpu.make_async_remote_copy(
            src_ref=wd_ref, dst_ref=wd.at[pl.ds(units, units)], send_sem=pair_send.at[1],
            recv_sem=pair_recv.at[1], device_id=sibling, device_id_type=MESH,
        ),
    ]
    local = [
        pltpu.make_async_copy(wgu_ref, wgu.at[0], local_sem.at[0]),
        pltpu.make_async_copy(wd_ref, wd.at[pl.ds(0, units)], local_sem.at[1]),
        pltpu.make_async_copy(x_ref, xg.at[0], local_sem.at[2]),
    ]
    for copy in pair + local:
        copy.start()

    def arrive(q, node):
        pltpu.make_async_copy(
            xg.at[SLOT[node], part(q)], xg.at[SLOT[node], part(q)], recv_sem.at[message(q, node)]
        ).wait()
        for child, way in CHILDREN.get((q, node), []):
            forward(xg.at[SLOT[node], part(q)], q, child, way).start()

    expert = lax.axis_index("ep")
    lane = lax.broadcasted_iota(jnp.int32, (GATE_LANES, GATE_LANES), 0)
    partner = expert + 1 - 2 * (expert % 2)

    def picker(which):
        hit = jnp.logical_and(lane % 32 == which, lane < 96)
        return jnp.where(hit, 1.0, 0.0).astype(jnp.bfloat16)

    pending = list(ARRIVALS)
    steps = []
    for step in range(16 // BLOCKS_PER_STEP):
        need = set(ORDER[step * BLOCKS_PER_STEP:(step + 1) * BLOCKS_PER_STEP])
        last = max([i for i, (q, node, _) in enumerate(pending) if node in need], default=-1)
        steps.append(pending[: last + 1])
        pending = pending[last + 1:]

    tile_rows = BLOCKS_PER_STEP * rows

    def step_body(step, carry):
        for index, events in enumerate(steps):
            if index == 0:
                @pl.when(step == 0)
                def _():
                    for copy in local:
                        copy.wait()
                    for copy in pair:
                        copy.wait()

            if events:
                @pl.when(step == index)
                def _(events=events):
                    for q, node, _ in events:
                        arrive(q, node)

        first = step * BLOCKS_PER_STEP
        x = xg[pl.ds(first, BLOCKS_PER_STEP), :, :width].reshape(tile_rows, width)
        lanes = xg[pl.ds(first, BLOCKS_PER_STEP), :, width:].reshape(tile_rows, GATE_LANES)
        for which in range(2):
            gate = jnp.dot(
                lanes, picker(expert if which == 0 else partner), preferred_element_type=jnp.float32
            )
            gate = jnp.concatenate([gate, gate], axis=1)
            for tile in range(units // 256):
                g = jnp.dot(
                    x, wgu[which, :, tile * 256:(tile + 1) * 256],
                    preferred_element_type=jnp.float32,
                )
                u = jnp.dot(
                    x, wgu[which, :, units + tile * 256:units + (tile + 1) * 256],
                    preferred_element_type=jnp.float32,
                )
                value = g / (1.0 + jnp.exp(-g)) * u * gate
                column = which * units + tile * 256
                hid[:, column:column + 256] = value.astype(jnp.bfloat16)
        hidden = hid[...]
        for tile in range(width // 256):
            columns = slice(tile * 256, (tile + 1) * 256)
            y = jnp.dot(hidden, wd[:, columns], preferred_element_type=jnp.float32)
            cbuf[pl.ds(first, BLOCKS_PER_STEP), :, columns] = y.astype(jnp.bfloat16).reshape(
                BLOCKS_PER_STEP, rows, 256
            )
        return carry

    lax.fori_loop(0, 16 // BLOCKS_PER_STEP, step_body, 0)

    def gathered(q, node):
        pltpu.make_async_copy(
            rbuf.at[message(q, node)], rbuf.at[message(q, node)], back_recv.at[message(q, node)]
        ).wait()

    for q, node, _ in reversed(ARRIVALS):
        own = cbuf.at[SLOT[node], part(q)]
        children = [message(q, child) for child, _ in CHILDREN.get((q, node), [])]
        for child, _ in CHILDREN.get((q, node), []):
            gathered(q, child)
        if children:
            def add(chunk, carry, own=own, children=children):
                piece = pl.ds(pl.multiple_of(chunk * 16, 16), 16)
                total = own[piece].astype(jnp.float32)
                for child in children:
                    total = total + rbuf[child, piece].astype(jnp.float32)
                own[piece] = total.astype(jnp.bfloat16)
                return carry

            lax.fori_loop(0, quarter_rows // 16, add, 0)
        _, way = tree_edge(q, node)
        pltpu.make_async_remote_copy(
            src_ref=own,
            dst_ref=rbuf.at[message(q, node)],
            send_sem=back_send,
            recv_sem=back_recv.at[message(q, node)],
            device_id=ways[way ^ 1],
            device_id_type=MESH,
        ).start()

    for q in range(4):
        children = [message(q, child) for child, _ in CHILDREN[(q, (0, 0))]]
        for child, _ in CHILDREN[(q, (0, 0))]:
            gathered(q, child)

        def finish(chunk, carry, q=q, children=children):
            piece = pl.ds(pl.multiple_of(chunk * 16, 16), 16)
            at = pl.ds(pl.multiple_of(q * quarter_rows + chunk * 16, 16), 16)
            total = res_ref[at] + cbuf[0, at].astype(jnp.float32)
            for child in children:
                total = total + rbuf[child, piece].astype(jnp.float32)
            out_ref[at] = total.astype(jnp.bfloat16)
            return carry

        lax.fori_loop(0, quarter_rows // 16, finish, 0)

    everything = xg.at[pl.ds(0, 15)]
    pltpu.make_async_copy(everything, everything, send_sem).wait()
    everything = cbuf.at[pl.ds(0, 15)]
    pltpu.make_async_copy(everything, everything, back_send).wait()


def experts(x, residual, gate_up, down):
    rows, width = residual.shape
    units = down.shape[0]
    return pl.pallas_call(
        experts_kernel,
        out_shape=jax.ShapeDtypeStruct((rows, width), jnp.bfloat16),
        in_specs=[
            pl.BlockSpec(memory_space=pltpu.VMEM),
            pl.BlockSpec(memory_space=pltpu.VMEM),
            pl.BlockSpec(memory_space=pl.ANY),
            pl.BlockSpec(memory_space=pl.ANY),
        ],
        out_specs=pl.BlockSpec(memory_space=pltpu.VMEM),
        scratch_shapes=[
            pltpu.VMEM((16, rows, width + GATE_LANES), jnp.bfloat16),
            pltpu.VMEM((16, rows, width), jnp.bfloat16),
            pltpu.VMEM((60, rows // 4, width), jnp.bfloat16),
            pltpu.VMEM((2, width, 2 * units), jnp.bfloat16),
            pltpu.VMEM((2 * units, width), jnp.bfloat16),
            pltpu.VMEM((BLOCKS_PER_STEP * rows, 2 * units), jnp.bfloat16),
            pltpu.SemaphoreType.DMA,
            pltpu.SemaphoreType.DMA((60,)),
            pltpu.SemaphoreType.DMA,
            pltpu.SemaphoreType.DMA((60,)),
            pltpu.SemaphoreType.DMA((3,)),
            pltpu.SemaphoreType.DMA((2,)),
            pltpu.SemaphoreType.DMA((2,)),
        ],
        compiler_params=pltpu.CompilerParams(
            collective_id=1, has_side_effects=True, vmem_limit_bytes=60 * 1024 * 1024
        ),
        name="experts",
    )(x, residual, gate_up, down)


def gate_lanes(expert_ids, gate_weights, expert_total):
    hit = expert_ids[:, :, None] == jnp.arange(expert_total, dtype=jnp.int32)[None, None, :]
    dense = jnp.sum(jnp.where(hit, gate_weights[:, :, None], 0.0), axis=1)
    high = lax.reduce_precision(dense, 8, 7)
    middle = lax.reduce_precision(dense - high, 8, 7)
    low = dense - high - middle
    spare = jnp.zeros((dense.shape[0], GATE_LANES - 3 * expert_total), jnp.float32)
    return jnp.concatenate([high, middle, low, spare], axis=1).astype(jnp.bfloat16)


def ancestry(parents):
    tree_width = parents.shape[-1]
    node_ids = jnp.arange(tree_width, dtype=jnp.int32)
    linked = jnp.logical_or(
        parents[..., :, None] == node_ids[None, :], node_ids[:, None] == node_ids[None, :]
    )
    closure = linked.astype(jnp.float32)
    for repeat in range(tree_width.bit_length()):
        closure = jnp.minimum(
            1.0, jnp.einsum("rij,rjk->rik", closure, closure, precision=lax.Precision.HIGHEST)
        )
    return closure > 0.5


def fold_block(running, scores, visible, product):
    highest, summed, gathered = running
    masked = jnp.where(visible[None], scores, NEG_FILL)
    updated = jnp.maximum(highest, jnp.max(masked, axis=-1))
    factor = jnp.exp(highest - updated)
    exp_weights = jnp.where(visible[None], jnp.exp(masked - updated[..., None]), 0.0)
    summed = summed * factor + jnp.sum(exp_weights, axis=-1)
    gathered = gathered * jnp.transpose(factor)[:, :, None] + product(
        exp_weights.astype(jnp.bfloat16)
    )
    return (updated, summed, gathered)


def per_device(
    hidden_in,
    tree_queries,
    tree_keys,
    tree_values,
    tree_parents,
    accepted_nodes,
    request_prompt,
    prompt_lengths,
    prompt_keys,
    prompt_values,
    out_proj,
    norm_gain,
    expert_ids,
    gate_weights,
    expert_gate_up,
    expert_down,
):
    tok_rows, feature_count = hidden_in.shape
    req_count, tree_len = tree_parents.shape
    prompt_count = prompt_keys.shape[0]
    score_scale = 1.0 / math.sqrt(HEAD_DIM)
    queries = tree_queries.reshape(tok_rows, HEADS, HEAD_DIM)
    own_keys = tree_keys.reshape(tok_rows, HEADS, HEAD_DIM)
    own_values = tree_values.reshape(tok_rows, HEADS, HEAD_DIM)
    token_request = jnp.arange(tok_rows, dtype=jnp.int32) // tree_len
    token_prompt = request_prompt[token_request]
    request_length = prompt_lengths[request_prompt]
    token_length = request_length[token_request]
    prompt_range = jnp.arange(prompt_count, dtype=jnp.int32)
    running = (
        jnp.full((HEADS, tok_rows), NEG_FILL, jnp.float32),
        jnp.zeros((HEADS, tok_rows), jnp.float32),
        jnp.zeros((tok_rows, HEADS, HEAD_DIM), jnp.float32),
    )
    page_keys = lax.all_gather(prompt_keys, "ep", axis=1, tiled=True)
    page_values = lax.all_gather(prompt_values, "ep", axis=1, tiled=True)
    rows_here = page_keys.shape[1]
    shaped_keys = page_keys.reshape(prompt_count, rows_here, HEADS, HEAD_DIM)
    flat_values = page_values.reshape(prompt_count * rows_here, HEADS, HEAD_DIM)
    scores = (
        jnp.einsum("thd,pkhd->htpk", queries, shaped_keys, preferred_element_type=jnp.float32)
        * score_scale
    )
    scores = scores.reshape(HEADS, tok_rows, prompt_count * rows_here)
    positions = jnp.arange(rows_here, dtype=jnp.int32)
    same_prompt = (token_prompt[:, None] == prompt_range[None, :])[:, :, None]
    in_length = (positions[None, :] < token_length[:, None])[:, None, :]
    visible = jnp.logical_and(same_prompt, in_length).reshape(tok_rows, prompt_count * rows_here)

    def product(weights):
        return jnp.einsum("htk,khd->thd", weights, flat_values, preferred_element_type=jnp.float32)

    running = fold_block(running, scores, visible, product)
    tree_seen = ancestry(tree_parents)
    node_index = jnp.arange(tok_rows, dtype=jnp.int32) % tree_len
    row_seen = tree_seen[token_request, node_index]
    same_request = token_request[:, None] == jnp.arange(req_count, dtype=jnp.int32)[None, :]
    tree_visible = jnp.logical_and(same_request[:, :, None], row_seen[:, None, :]).reshape(
        tok_rows, tok_rows
    )
    tree_scores = (
        jnp.einsum("thd,khd->htk", queries, own_keys, preferred_element_type=jnp.float32)
        * score_scale
    )

    def tree_product(weights):
        return jnp.einsum("htk,khd->thd", weights, own_values, preferred_element_type=jnp.float32)

    highest, summed, gathered = fold_block(running, tree_scores, tree_visible, tree_product)
    attended = (
        (gathered / jnp.transpose(summed)[:, :, None])
        .reshape(tok_rows, feature_count)
        .astype(jnp.bfloat16)
    )
    projected = jnp.dot(
        attended,
        lax.all_gather(out_proj, "rep", axis=0, tiled=True),
        preferred_element_type=jnp.float32,
    )
    residual = hidden_in.astype(jnp.float32) + projected
    normed = (
        residual
        * lax.rsqrt(jnp.mean(residual * residual, axis=-1, keepdims=True) + EPSILON)
        * norm_gain
    ).astype(jnp.bfloat16)
    x = jnp.concatenate(
        [normed, gate_lanes(expert_ids, gate_weights, lax.axis_size("ep"))], axis=1
    )
    layer_out = experts(x, residual, expert_gate_up[0], expert_down[0])
    accepted_rows = jnp.arange(req_count, dtype=jnp.int32)[:, None] * tree_len + accepted_nodes
    accepted_cache = jnp.concatenate(
        [tree_keys[accepted_rows], tree_values[accepted_rows]], axis=-1
    )
    return (layer_out, accepted_cache)


def solution(mesh):
    in_specs = (
        P(("rep", "ep"), None),
        P(("rep", "ep"), None),
        P(("rep", "ep"), None),
        P(("rep", "ep"), None),
        P(("rep", "ep"), None),
        P(("rep", "ep"), None),
        P(("rep", "ep")),
        P("rep"),
        P("rep", "ep", None),
        P("rep", "ep", None),
        P("rep", None),
        P(),
        P(("rep", "ep"), None),
        P(("rep", "ep"), None),
        P("ep", None, None),
        P("ep", None, None),
    )
    out_specs = (P(("rep", "ep"), None), P(("rep", "ep"), None, None))
    return jax.shard_map(
        per_device, mesh=mesh, in_specs=in_specs, out_specs=out_specs, check_vma=False
    )
```
